32 devices in a mesh: row: 8 (over y, x, core), col: 4 (over z).
Axes of the slice: x: 2, y: 2, z: 4, core: 2. Of those that a mesh axis runs over, the one named last changes fastest.
Arguments:
- block_input: bfloat16 [8192, 768], P(('row', 'col'))
- block_cotangent: bfloat16 [8192, 768], P(('row', 'col')), may hold values from -6 to 6
- block_lengths: int32 [64], P(('row', 'col')), may hold values from 1 to 128, as said below
- block_offsets: int32 [64], P(('row', 'col')), may hold values from 0 to 128, as said below
- norm1_gain: float32 [768], replicated, may hold values from 0.25 to 1.75
- norm1_bias: float32 [768], replicated, may hold values from -2.5 to 2.5
- norm2_gain: float32 [768], replicated, may hold values from 0.25 to 1.75
- norm2_bias: float32 [768], replicated, may hold values from -2.5 to 2.5
- qkv_weight: bfloat16 [768, 2304], P('row', 'col'), may hold values from -0.21875 to 0.21875
- qkv_bias: float32 [2304], P('col'), may hold values from -3 to 3
- dense_weight: bfloat16 [768, 768], P('col', 'row'), may hold values from -0.875 to 0.875
- dense_bias: float32 [768], replicated, may hold values from -2.5 to 2.5
- fc_in_weight: bfloat16 [768, 3072], P('row', 'col'), may hold values from -0.21875 to 0.21875
- fc_in_bias: float32 [3072], P('col'), may hold values from -3 to 3
- fc_out_weight: bfloat16 [3072, 768], P('col', 'row'), may hold values from -0.109375 to 0.109375
- fc_out_bias: float32 [768], replicated, may hold values from -2.5 to 2.5
Outputs:
- block_out: float32 [8192, 768], P(('row', 'col'))
- input_grad: float32 [8192, 768], P(('row', 'col'))
- norm1_gain_grad: float32 [768], replicated
- norm1_bias_grad: float32 [768], replicated
- norm2_gain_grad: float32 [768], replicated
- norm2_bias_grad: float32 [768], replicated
- qkv_weight_grad: float32 [768, 2304], P('row', 'col')
- qkv_bias_grad: float32 [2304], P('col')
- dense_weight_grad: float32 [768, 768], P('col', 'row')
- dense_bias_grad: float32 [768], replicated
- fc_in_weight_grad: float32 [768, 3072], P('row', 'col')
- fc_in_bias_grad: float32 [3072], P('col')
- fc_out_weight_grad: float32 [3072, 768], P('col', 'row')
- fc_out_bias_grad: float32 [768], replicated
The draws below stay inside these ranges and needn't reach their ends.
Inputs may be any that keep to these rules, and one draw needn't show every extreme that they name: `block_lengths`: blocks come in aligned pairs. A pair holds either two sequences, each in its own block, or one sequence over both blocks, whose first block is then full. `block_offsets`: an even block's offset is 0; an odd block's is 0 when it starts a sequence and 128 when it continues the sequence of the block before it.
All inputs are finite; a program needn't handle non-finite values.
Results may differ from the reference program's by a relative error of at most 0.0088.
Values may be sent and summed in bfloat16 or wider, within the bound.
A program may use at most 128 MiB of HBM per device.

```python
import math
import jax
import jax.numpy as jnp
from jax import lax

D = 768
HEADS = 12
HD = 64
ROT = 16
FF = 3072
BLK = 128
TOKENS = 8192
BLOCKS = 64
GROUPS = 4


def block_layout(key):
    folded = jax.random.fold_in(key, 11)
    joined = jax.random.randint(jax.random.fold_in(folded, 1), (BLOCKS // 2,), 0, 2)
    joined = joined.at[0].set(1)
    counts = jax.random.randint(jax.random.fold_in(folded, 2), (BLOCKS // 2, 2), 1, BLK + 1)
    counts = counts.at[0, 1].set(BLK)
    leading = jnp.where(joined == 1, BLK, counts[:, 0])
    lengths = jnp.stack([leading, counts[:, 1]], axis=1).reshape(-1).astype(jnp.int32)
    offsets = jnp.stack([jnp.zeros_like(joined), joined * BLK], axis=1).reshape(-1).astype(jnp.int32)
    return (lengths, offsets)


def draw_block_lengths(key, part):
    return block_layout(key)[0]


def draw_block_offsets(key, part):
    return block_layout(key)[1]


def draw_block_input(key, part):
    row_key = jax.random.fold_in(key, 21)
    col_key = jax.random.fold_in(key, 22)
    base_key = jax.random.fold_in(key, 23)
    row_scale = jnp.exp(jax.random.uniform(row_key, (TOKENS, 1), jnp.float32, math.log(0.3), math.log(3.0)))
    col_scale = jnp.exp(jax.random.uniform(col_key, (1, D), jnp.float32, math.log(0.3), math.log(3.0)))
    values = jax.random.normal(base_key, (TOKENS, D), jnp.float32)
    return (values * row_scale * col_scale).astype(jnp.bfloat16)


def strengthened(drawn, own_key, source, target, parts, factor):
    owner, partner = [(jnp.arange(drawn.shape[axis_at]) // (drawn.shape[axis_at] // parts)).reshape([-1 if axis == axis_at else 1 for axis in range(drawn.ndim)]) for axis_at in (source, target)]
    chosen = jax.random.permutation(own_key, parts)[partner]
    strong = (owner == chosen) | (owner == (partner + parts // 2) % parts)
    return jnp.where(strong, factor * drawn, drawn)


def levels(key, shape, cuts, smallest, high):
    level = 1.0
    for dim, shards_of in cuts:
        heights = jax.random.uniform(jax.random.fold_in(jax.random.fold_in(key, 6), dim), (shards_of,), jnp.float32, smallest / len(cuts), high / len(cuts))
        level = level * jnp.repeat(jnp.exp(heights), shape[dim] // shards_of).reshape((-1,) + (1,) * (len(shape) - 1 - dim))
    return level


def bell_draw(stream_key, shape, scale, reach, split=(), held_as=jnp.bfloat16):
    values = jax.random.normal(stream_key, shape, jnp.float32) * scale
    if len(split) > 0:
        values = levels(stream_key, shape, split, -0.22, 0.18) * values
    return jnp.clip(values, min=-reach, max=reach).astype(held_as)


def bell_draw_with(stream_key, extent, deviation, limit, split, heavy, kind=jnp.bfloat16):
    result = deviation * jax.random.normal(stream_key, extent, jnp.float32)
    if split:
        result = result * levels(stream_key, extent, split, -0.22, 0.18)
    return jnp.clip(strengthened(result, jax.random.fold_in(stream_key, 3), *heavy), -limit, limit).astype(kind)


def setup_inputs(seed: int = 0) -> dict:
    key_of = jax.random.split(jax.random.key(seed), 17)
    block_input = draw_block_input(jax.random.fold_in(key_of[16], 71), 0)
    block_cotangent = bell_draw_with(key_of[1], (TOKENS, D), 1.0, 6.0, ((0, 32),), (0, 1, 32, 2.75))
    block_lengths = draw_block_lengths(jax.random.fold_in(key_of[16], 71), 0)
    block_offsets = draw_block_offsets(jax.random.fold_in(key_of[16], 71), 0)
    norm1_gain = jnp.clip(1.0 + 0.15 * jax.random.normal(key_of[4], (D,), jnp.float32), 0.25, 1.75)
    norm1_bias = bell_draw(key_of[5], (D,), 0.3, 2.5, (), jnp.float32)
    norm2_gain = jnp.clip(1.0 + 0.15 * jax.random.normal(key_of[6], (D,), jnp.float32), 0.25, 1.75)
    norm2_bias = bell_draw(key_of[7], (D,), 0.3, 2.5, (), jnp.float32)
    qkv_weight = bell_draw(key_of[8], (D, 3 * D), D ** -0.5, 0.21875, ((0, 8), (1, 4)))
    qkv_bias = bell_draw(key_of[9], (3 * D,), 0.5, 3.0, ((0, 4),), jnp.float32)
    dense_weight = bell_draw(key_of[10], (D, D), (D // 16) ** -0.5, 0.875, ((0, 4), (1, 8)))
    dense_bias = bell_draw(key_of[11], (D,), 0.3, 2.5, (), jnp.float32)
    fc_in_weight = bell_draw(key_of[12], (D, FF), D ** -0.5, 0.21875, ((0, 8), (1, 4)))
    fc_in_bias = bell_draw(key_of[13], (FF,), 0.5, 3.0, ((0, 4),), jnp.float32)
    fc_out_weight = bell_draw(key_of[14], (FF, D), FF ** -0.5, 0.109375, ((0, 4), (1, 8)))
    fc_out_bias = bell_draw(key_of[15], (D,), 0.3, 2.5, (), jnp.float32)
    return {"block_input": block_input, "block_cotangent": block_cotangent, "block_lengths": block_lengths, "block_offsets": block_offsets, "norm1_gain": norm1_gain, "norm1_bias": norm1_bias, "norm2_gain": norm2_gain, "norm2_bias": norm2_bias, "qkv_weight": qkv_weight, "qkv_bias": qkv_bias, "dense_weight": dense_weight, "dense_bias": dense_bias, "fc_in_weight": fc_in_weight, "fc_in_bias": fc_in_bias, "fc_out_weight": fc_out_weight, "fc_out_bias": fc_out_bias}


NORM_EPSILON = 1e-05
HALF_ROOT = math.sqrt(0.5)
DENSITY_SCALE = 1.0 / math.sqrt(2.0 * math.pi)

def normalize(features):
    widened = features.astype(jnp.float32)
    centered = widened - lax.optimization_barrier(jnp.mean(widened, axis=1, keepdims=True))
    inverse = lax.rsqrt(lax.optimization_barrier(jnp.mean(centered * centered, axis=1, keepdims=True)) + NORM_EPSILON)
    return (centered * inverse, inverse)

def norm_back(grad_normed, gain, standard, inverse):
    grad_unit = grad_normed * gain
    return inverse * (grad_unit - lax.optimization_barrier(jnp.mean(grad_unit, axis=1, keepdims=True)) - standard * lax.optimization_barrier(jnp.mean(grad_unit * standard, axis=1, keepdims=True)))

def gelu_exact(pre_act):
    return 0.5 * pre_act * (1.0 + lax.erf(pre_act * HALF_ROOT))

def gelu_slope(pre_act):
    return 0.5 * (1.0 + lax.erf(pre_act * HALF_ROOT)) + pre_act * jnp.exp(-0.5 * pre_act * pre_act) * DENSITY_SCALE

def rotary_tables(positions, rotated):
    halves = rotated // 2
    frequency = 10000.0 ** (-2.0 * jnp.arange(halves, dtype=jnp.float32) / rotated)
    angles = positions[:, None].astype(jnp.float32) * frequency[None, :]
    angles = jnp.concatenate([angles, angles], axis=1)
    return (jnp.cos(angles)[:, None, :], jnp.sin(angles)[:, None, :])

def rotate(values, cosine, sine_table, rotated):
    halves = rotated // 2
    leading = values[..., :rotated]
    turned = jnp.concatenate([-leading[..., halves:], leading[..., :halves]], axis=-1)
    return jnp.concatenate([leading * cosine + turned * sine_table, values[..., rotated:]], axis=-1)

def unrotate(gradient, cosine, sine_table, rotated):
    halves = rotated // 2
    leading = gradient[..., :rotated]
    scaled = leading * sine_table
    turned = jnp.concatenate([scaled[..., halves:], -scaled[..., :halves]], axis=-1)
    return jnp.concatenate([leading * cosine + turned, gradient[..., rotated:]], axis=-1)

def pair_mask(lengths, offsets, block_rows):
    pair_count = lengths.shape[0] // 2
    local_rows = jnp.arange(2 * block_rows, dtype=jnp.int32)
    block_of = local_rows // block_rows
    in_block = local_rows % block_rows
    pair_lengths = lengths.reshape(pair_count, 2)
    joined = offsets.reshape(pair_count, 2)[:, 1] > 0
    row_limit = jnp.where(block_of[None, :] == 0, pair_lengths[:, 0:1], pair_lengths[:, 1:2])
    live_keys = in_block[None, :] < row_limit
    same_seq = (block_of[:, None] == block_of[None, :])[None, :, :] | joined[:, None, None]
    causal = (local_rows[None, :] <= local_rows[:, None])[None, :, :]
    diagonal = (local_rows[:, None] == local_rows[None, :])[None, :, :]
    return same_seq & causal & (live_keys[:, None, :] | diagonal)

def attend(queries, key_rows, values, allowed, score_scale):
    scores = jnp.einsum('pihd,pjhd->phij', queries.astype(jnp.float32), key_rows.astype(jnp.float32)) * score_scale
    scores = jnp.where(allowed[:, None, :, :], scores, -jnp.inf)
    highest = lax.optimization_barrier(jnp.max(scores, axis=-1, keepdims=True))
    totals = highest + jnp.log(lax.optimization_barrier(jnp.sum(jnp.exp(scores - highest), axis=-1, keepdims=True)))
    weights = jnp.exp(scores - totals).astype(jnp.bfloat16)
    attended = jnp.einsum('phij,pjhd->pihd', weights.astype(jnp.float32), values.astype(jnp.float32))
    return (attended.astype(jnp.bfloat16), totals)

def attend_back(queries, key_rows, values, allowed, totals, grad_att, score_scale):
    scores = jnp.einsum('pihd,pjhd->phij', queries.astype(jnp.float32), key_rows.astype(jnp.float32)) * score_scale
    scores = jnp.where(allowed[:, None, :, :], scores, -jnp.inf)
    probability = jnp.exp(scores - totals)
    weights = probability.astype(jnp.bfloat16)
    grad_probs = jnp.einsum('pihd,pjhd->phij', grad_att.astype(jnp.float32), values.astype(jnp.float32))
    row_dot = lax.optimization_barrier(jnp.sum(probability * grad_probs, axis=-1, keepdims=True))
    grad_scores = (probability * (grad_probs - row_dot) * score_scale).astype(jnp.bfloat16)
    wide_scores = grad_scores.astype(jnp.float32)
    grad_query = jnp.einsum('phij,pjhd->pihd', wide_scores, key_rows.astype(jnp.float32))
    grad_key = jnp.einsum('phij,pihd->pjhd', wide_scores, queries.astype(jnp.float32))
    grad_values = jnp.einsum('phij,pihd->pjhd', weights.astype(jnp.float32), grad_att.astype(jnp.float32))
    return (grad_query, grad_key, grad_values.astype(jnp.bfloat16))

def reference(block_input, block_cotangent, block_lengths, block_offsets, norm1_gain, norm1_bias, norm2_gain, norm2_bias, qkv_weight, qkv_bias, dense_weight, dense_bias, fc_in_weight, fc_in_bias, fc_out_weight, fc_out_bias):
    step_rows = math.gcd(TOKENS, 4096)
    step_count = TOKENS // step_rows
    step_blocks = step_rows // BLK
    pair_count = step_rows // (2 * BLK)
    score_scale = HD ** (-0.5)
    att_cols = D // GROUPS
    ff_cols = FF // GROUPS
    dense_wide = dense_weight.astype(jnp.float32).reshape(GROUPS, att_cols, D)
    fc_out_wide = fc_out_weight.astype(jnp.float32).reshape(GROUPS, ff_cols, D)
    in_block = jnp.arange(BLK, dtype=jnp.int32)
    four_shape = (pair_count, 2 * BLK, HEADS, HD)

    def advance(running, pieces):
        inputs, cotangent, lengths, offsets = pieces
        standard, inverse = normalize(inputs)
        normed_first = (standard * norm1_gain + norm1_bias).astype(jnp.bfloat16)
        normed_second = (standard * norm2_gain + norm2_bias).astype(jnp.bfloat16)
        positions = (offsets[:, None] + in_block[None, :]).reshape(-1).astype(jnp.int32)
        valid = (in_block[None, :] < lengths[:, None]).reshape(-1)
        cosine, sine_table = rotary_tables(positions, ROT)
        allowed = pair_mask(lengths, offsets, BLK)
        mixed_cols = (jnp.dot(normed_first, qkv_weight, preferred_element_type=jnp.float32) + qkv_bias).astype(jnp.bfloat16)
        mixed_cols = mixed_cols.reshape(step_rows, 3, HEADS, HD)
        queries = rotate(mixed_cols[:, 0].astype(jnp.float32), cosine, sine_table, ROT).astype(jnp.bfloat16)
        key_rows = rotate(mixed_cols[:, 1].astype(jnp.float32), cosine, sine_table, ROT).astype(jnp.bfloat16)
        values = mixed_cols[:, 2]
        queries = queries.reshape(four_shape)
        key_rows = key_rows.reshape(four_shape)
        values = values.reshape(four_shape)
        attended, totals = attend(queries, key_rows, values, allowed, score_scale)
        attended = attended.reshape(step_rows, D)
        pre_act = jnp.dot(normed_second, fc_in_weight, preferred_element_type=jnp.float32) + fc_in_bias
        hidden = gelu_exact(pre_act).astype(jnp.bfloat16)
        partial_value = jnp.einsum('rck,ckd->rcd', attended.astype(jnp.float32).reshape(step_rows, GROUPS, att_cols), dense_wide) + jnp.einsum('rck,ckd->rcd', hidden.astype(jnp.float32).reshape(step_rows, GROUPS, ff_cols), fc_out_wide)
        partial_value = lax.optimization_barrier(partial_value.astype(jnp.bfloat16))
        output = inputs.astype(jnp.float32) + dense_bias + fc_out_bias + lax.optimization_barrier(jnp.sum(partial_value.astype(jnp.float32), axis=1))
        grad_out = jnp.where(valid[:, None], cotangent, jnp.zeros_like(cotangent))
        grad_hidden = jnp.dot(grad_out, fc_out_weight.T, preferred_element_type=jnp.float32)
        grad_pre = (grad_hidden * gelu_slope(pre_act)).astype(jnp.bfloat16)
        grad_att = jnp.dot(grad_out, dense_weight.T, preferred_element_type=jnp.float32).astype(jnp.bfloat16)
        grad_query, grad_key, grad_values = attend_back(queries, key_rows, values, allowed, totals, grad_att.reshape(four_shape), score_scale)
        grad_query = unrotate(grad_query.reshape(step_rows, HEADS, HD), cosine, sine_table, ROT).astype(jnp.bfloat16)
        grad_key = unrotate(grad_key.reshape(step_rows, HEADS, HD), cosine, sine_table, ROT).astype(jnp.bfloat16)
        grad_mixed = jnp.stack([grad_query, grad_key, grad_values.reshape(step_rows, HEADS, HD)], axis=1)
        grad_mixed = grad_mixed.reshape(step_rows, 3 * D)
        back_first = jnp.dot(grad_mixed, qkv_weight.T, preferred_element_type=jnp.float32)
        back_second = jnp.dot(grad_pre, fc_in_weight.T, preferred_element_type=jnp.float32)
        input_grad = grad_out.astype(jnp.float32) + norm_back(back_first, norm1_gain, standard, inverse) + norm_back(back_second, norm2_gain, standard, inverse)
        acc_qkv_w, acc_qkv_b, acc_dense_w, acc_out_b, acc_in_w, acc_in_b, acc_out_w, acc_gain_one, acc_bias_one, acc_gain_two, acc_bias_two = running
        acc_qkv_w = acc_qkv_w + jnp.dot(normed_first.T, grad_mixed, preferred_element_type=jnp.float32)
        acc_qkv_b = acc_qkv_b + lax.optimization_barrier(jnp.sum(grad_mixed.astype(jnp.float32), axis=0))
        acc_dense_w = acc_dense_w + jnp.dot(attended.T, grad_out, preferred_element_type=jnp.float32)
        acc_out_b = acc_out_b + lax.optimization_barrier(jnp.sum(grad_out.astype(jnp.float32), axis=0))
        acc_in_w = acc_in_w + jnp.dot(normed_second.T, grad_pre, preferred_element_type=jnp.float32)
        acc_in_b = acc_in_b + lax.optimization_barrier(jnp.sum(grad_pre.astype(jnp.float32), axis=0))
        acc_out_w = acc_out_w + jnp.dot(hidden.T, grad_out, preferred_element_type=jnp.float32)
        acc_gain_one = acc_gain_one + lax.optimization_barrier(jnp.sum(back_first * standard, axis=0))
        acc_bias_one = acc_bias_one + lax.optimization_barrier(jnp.sum(back_first, axis=0))
        acc_gain_two = acc_gain_two + lax.optimization_barrier(jnp.sum(back_second * standard, axis=0))
        acc_bias_two = acc_bias_two + lax.optimization_barrier(jnp.sum(back_second, axis=0))
        running = (acc_qkv_w, acc_qkv_b, acc_dense_w, acc_out_b, acc_in_w, acc_in_b, acc_out_w, acc_gain_one, acc_bias_one, acc_gain_two, acc_bias_two)
        return (running, (output, input_grad))
    start_state = (jnp.zeros((D, 3 * D), jnp.float32), jnp.zeros((3 * D,), jnp.float32), jnp.zeros((D, D), jnp.float32), jnp.zeros((D,), jnp.float32), jnp.zeros((D, FF), jnp.float32), jnp.zeros((FF,), jnp.float32), jnp.zeros((FF, D), jnp.float32), jnp.zeros((D,), jnp.float32), jnp.zeros((D,), jnp.float32), jnp.zeros((D,), jnp.float32), jnp.zeros((D,), jnp.float32))
    pieces = (block_input.reshape(step_count, step_rows, D), block_cotangent.reshape(step_count, step_rows, D), block_lengths.reshape(step_count, step_blocks), block_offsets.reshape(step_count, step_blocks))
    running, stacked = lax.scan(advance, start_state, pieces)
    acc_qkv_w, acc_qkv_b, acc_dense_w, acc_out_b, acc_in_w, acc_in_b, acc_out_w, acc_gain_one, acc_bias_one, acc_gain_two, acc_bias_two = running
    block_out = stacked[0].reshape(TOKENS, D)
    input_grad = stacked[1].reshape(TOKENS, D)
    return (block_out, input_grad, acc_gain_one, acc_bias_one, acc_gain_two, acc_bias_two, acc_qkv_w, acc_qkv_b, acc_dense_w, acc_out_b, acc_in_w, acc_in_b, acc_out_w, acc_out_b)
```

```python
import math

import jax
import jax.numpy as jnp
from jax import lax
from jax.experimental import pallas as pl
from jax.experimental.pallas import tpu as pltpu
from jax.sharding import PartitionSpec as P

HEADS = 12
ROT = 16


NORM_EPSILON = 1e-05
HALF_ROOT = math.sqrt(0.5)
DENSITY_SCALE = 1.0 / math.sqrt(2.0 * math.pi)


def normalize(features):
    widened = features.astype(jnp.float32)
    centered = widened - jnp.mean(widened, axis=1, keepdims=True)
    inverse = lax.rsqrt(jnp.mean(centered * centered, axis=1, keepdims=True) + NORM_EPSILON)
    return (centered * inverse, inverse)


def norm_back(grad_normed, gain, standard, inverse):
    grad_unit = grad_normed * gain
    return inverse * (
        grad_unit
        - jnp.mean(grad_unit, axis=1, keepdims=True)
        - standard * jnp.mean(grad_unit * standard, axis=1, keepdims=True)
    )


def gelu_exact(pre_act):
    return 0.5 * pre_act * (1.0 + lax.erf(pre_act * HALF_ROOT))


def gelu_slope(pre_act):
    return (
        0.5 * (1.0 + lax.erf(pre_act * HALF_ROOT))
        + pre_act * jnp.exp(-0.5 * pre_act * pre_act) * DENSITY_SCALE
    )


def rotary_tables(positions, rotated):
    halves = rotated // 2
    frequency = 10000.0 ** (-2.0 * jnp.arange(halves, dtype=jnp.float32) / rotated)
    angles = positions[:, None].astype(jnp.float32) * frequency[None, :]
    angles = jnp.concatenate([angles, angles], axis=1)
    return (jnp.cos(angles)[:, None, :], jnp.sin(angles)[:, None, :])


def rotate(values, cosine, sine_table, rotated):
    halves = rotated // 2
    leading = values[..., :rotated]
    turned = jnp.concatenate([-leading[..., halves:], leading[..., :halves]], axis=-1)
    return jnp.concatenate([leading * cosine + turned * sine_table, values[..., rotated:]], axis=-1)


def unrotate(gradient, cosine, sine_table, rotated):
    halves = rotated // 2
    leading = gradient[..., :rotated]
    scaled = leading * sine_table
    turned = jnp.concatenate([scaled[..., halves:], -scaled[..., :halves]], axis=-1)
    return jnp.concatenate([leading * cosine + turned, gradient[..., rotated:]], axis=-1)


def pair_mask(lengths, offsets, block_rows):
    pair_count = lengths.shape[0] // 2
    local_rows = jnp.arange(2 * block_rows, dtype=jnp.int32)
    block_of = local_rows // block_rows
    in_block = local_rows % block_rows
    pair_lengths = lengths.reshape(pair_count, 2)
    joined = offsets.reshape(pair_count, 2)[:, 1] > 0
    row_limit = jnp.where(block_of[None, :] == 0, pair_lengths[:, 0:1], pair_lengths[:, 1:2])
    live_keys = in_block[None, :] < row_limit
    same_seq = (block_of[:, None] == block_of[None, :])[None, :, :] | joined[:, None, None]
    causal = (local_rows[None, :] <= local_rows[:, None])[None, :, :]
    diagonal = (local_rows[:, None] == local_rows[None, :])[None, :, :]
    return same_seq & causal & (live_keys[:, None, :] | diagonal)


def masked_scores(queries, key_rows, allowed, score_scale):
    scores = (
        jnp.einsum("pihd,pjhd->phij", queries, key_rows, preferred_element_type=jnp.float32)
        * score_scale
    )
    return jnp.where(allowed[:, None, :, :], scores, -jnp.inf)


MESH = pl.DeviceIdType.MESH
RING_ROWS = 8
RING_COLS = 4


def partners():
    row = lax.axis_index("row")
    col = lax.axis_index("col")
    beside = row + 1 - 2 * (row % 2)
    across = row + 2 - 4 * ((row // 2) % 2)
    above = row + 4 - 8 * (row // 4)
    return row, col, beside, across, above


def greet(row, col, beside, across, above):
    barrier = pltpu.get_barrier_semaphore()
    others = [(beside, col), (across, col), (above, col)]
    others += [(row, (col + step) % RING_COLS) for step in range(1, RING_COLS)]
    for other in others:
        pl.semaphore_signal(barrier, inc=1, device_id=other, device_id_type=MESH)
    pl.semaphore_wait(barrier, len(others))


class Sends:
    def __init__(self, send_sems, recv_sems):
        self.send_sems = send_sems
        self.recv_sems = recv_sems
        self.copies = {}

    def start(self, name, source, target, device):
        at = len(self.copies)
        copy = pltpu.make_async_remote_copy(
            src_ref=source,
            dst_ref=target,
            send_sem=self.send_sems.at[at],
            recv_sem=self.recv_sems.at[at],
            device_id=device,
            device_id_type=MESH,
        )
        copy.start()
        self.copies[name] = copy

    def arrived(self, name):
        self.copies[name].wait_recv()

    def finish(self):
        for copy in self.copies.values():
            copy.wait_send()


GATHER_COPIES = 39


def gather_kernel(shard, out, own_sem, send_sems, recv_sems):
    row, col, beside, across, above = partners()
    diagonal = across + 4 - 8 * (across // 4)
    half = shard.shape[0] // 2
    low, high = pl.ds(0, half), pl.ds(half, half)
    greet(row, col, beside, across, above)
    sends = Sends(send_sems, recv_sems)
    own = pltpu.make_async_copy(shard, out.at[col, row], own_sem)
    own.start()

    def share(step):
        at = (col - step + RING_COLS) % RING_COLS
        piece = shard if step == 0 else out.at[at, row]
        sends.start(("x", step), piece, out.at[at, row], (across, col))
        sends.start(("y", step), piece, out.at[at, row], (above, col))
        if step == 0:
            for hop in (1, 2, 3):
                there = (col + hop) % RING_COLS
                sends.start(("z", hop), shard, out.at[col, row], (row, there))
        sends.start(("c", step), piece, out.at[at, row], (beside, col))

    def relay(step):
        at = (col - step + RING_COLS) % RING_COLS
        sends.arrived(("x", step))
        sends.start(("dy", step), out.at[at, across, high], out.at[at, across, high], (above, col))
        sends.start(("cx", step), out.at[at, across], out.at[at, across], (beside, col))
        sends.arrived(("y", step))
        sends.start(("dx", step), out.at[at, above, low], out.at[at, above, low], (across, col))
        sends.start(("cy", step), out.at[at, above], out.at[at, above], (beside, col))

    def close(step):
        at = (col - step + RING_COLS) % RING_COLS
        sends.arrived(("dx", step))
        sends.start(("cdx", step), out.at[at, diagonal, low], out.at[at, diagonal, low], (beside, col))
        sends.arrived(("dy", step))
        sends.start(("cdy", step), out.at[at, diagonal, high], out.at[at, diagonal, high], (beside, col))

    share(0)
    sends.arrived(("z", 1))
    share(1)
    relay(0)
    sends.arrived(("z", 2))
    share(2)
    relay(1)
    close(0)
    sends.arrived(("z", 3))
    share(3)
    relay(2)
    close(1)
    relay(3)
    close(2)
    close(3)
    for step in range(RING_COLS):
        for kind in ("c", "cx", "cy", "cdx", "cdy"):
            sends.arrived((kind, step))
    sends.finish()
    own.wait()


def gather_shards(shard, rows, cols):
    if (rows, cols) != (RING_ROWS, RING_COLS):
        return lax.all_gather(shard, ("col", "row"), axis=0, tiled=True).reshape(
            cols, rows * shard.shape[0], shard.shape[1]
        )
    gathered = pl.pallas_call(
        gather_kernel,
        out_shape=jax.ShapeDtypeStruct((cols, rows) + shard.shape, shard.dtype),
        in_specs=[pl.BlockSpec(memory_space=pl.ANY)],
        out_specs=pl.BlockSpec(memory_space=pl.ANY),
        scratch_shapes=[
            pltpu.SemaphoreType.DMA,
            pltpu.SemaphoreType.DMA((GATHER_COPIES,)),
            pltpu.SemaphoreType.DMA((GATHER_COPIES,)),
        ],
        compiler_params=pltpu.CompilerParams(collective_id=0, has_side_effects=True),
    )(shard)
    return gathered.reshape(cols, rows * shard.shape[0], shard.shape[1])


SCATTER_COPIES = 40


def add_rows(target, source, start, count):
    @pl.loop(0, count // 16)
    def _(tile):
        rows = pl.ds(pl.multiple_of(start + tile * 16, 16), 16)
        target[rows, :] = (
            target[rows, :].astype(jnp.float32) + source[rows, :].astype(jnp.float32)
        ).astype(target.dtype)


SELF, ACROSS, ABOVE, DIAGONAL = range(4)


def scatter_kernel(
    grads,
    small,
    out,
    small_out,
    total,
    from_core,
    from_x,
    from_y,
    diag_x,
    diag_y,
    from_z,
    small_in,
    small_sum,
    own_sems,
    send_sems,
    recv_sems,
):
    row, col, beside, across, above = partners()
    diagonal = across + 4 - 8 * (across // 4)
    chips = (row, across, above, diagonal)
    height = out.shape[0]
    half = height // 2
    low, high = pl.ds(0, half), pl.ds(half, half)
    order = (1, 2, 3, 0)
    places = (DIAGONAL, ACROSS, ABOVE, SELF)
    greet(row, col, beside, across, above)
    sends = Sends(send_sems, recv_sems)
    next_col = col + 1 - 2 * (col % 2)
    far_col = col + 2 - 4 * (col // 2)
    small_targets = ((beside, col), (across, col), (above, col), (row, next_col), (row, far_col))

    def send_small(stage):
        sends.start(("s", stage), small_sum.at[stage], small_in.at[stage], small_targets[stage])

    def fold_small(stage):
        sends.arrived(("s", stage))
        summed = small_sum[stage] + small_in[stage]
        if stage + 1 < len(small_targets):
            small_sum[stage + 1] = summed
            send_small(stage + 1)
        else:
            small_out[...] = summed

    small_sum[0] = small[...]
    loads = {}
    for step in order:
        at = (col + step) % RING_COLS
        for place in places:
            chip = chips[place]
            other = chip + 1 - 2 * (chip % 2)
            sends.start(
                ("c", step, place), grads.at[at, other], from_core.at[step, place], (beside, col)
            )
            load = pltpu.make_async_copy(
                grads.at[at, chip], total.at[step, place], own_sems.at[step * 4 + place]
            )
            load.start()
            loads[step, place] = load
    send_small(0)

    def pair(step):
        for place in places:
            loads[step, place].wait()
            sends.arrived(("c", step, place))
            add_rows(total.at[step, place], from_core.at[step, place], 0, height)
            if place == DIAGONAL:
                sends.start(
                    ("dx", step), total.at[step, DIAGONAL, low], diag_x.at[step, low], (across, col)
                )
                sends.start(
                    ("dy", step), total.at[step, DIAGONAL, high], diag_y.at[step, high], (above, col)
                )

    def turn(step):
        sends.arrived(("dx", step))
        add_rows(total.at[step, ABOVE], diag_x.at[step], 0, half)
        sends.start(("y", step), total.at[step, ABOVE], from_y.at[step], (above, col))
        sends.arrived(("dy", step))
        add_rows(total.at[step, ACROSS], diag_y.at[step], half, half)
        sends.start(("x", step), total.at[step, ACROSS], from_x.at[step], (across, col))

    def leave(step):
        sends.arrived(("x", step))
        add_rows(total.at[step, SELF], from_x.at[step], 0, height)
        sends.arrived(("y", step))
        add_rows(total.at[step, SELF], from_y.at[step], 0, height)
        if step > 0:
            there = (col + step) % RING_COLS
            sends.start(("z", step), total.at[step, SELF], from_z.at[step - 1], (row, there))

    for turn_at in range(len(order) + 2):
        if turn_at < len(order):
            pair(order[turn_at])
        if 1 <= turn_at <= len(order):
            turn(order[turn_at - 1])
        if turn_at >= 2:
            leave(order[turn_at - 2])
        if turn_at < len(small_targets):
            fold_small(turn_at)
    for step in (1, 2, 3):
        sends.arrived(("z", step))

    @pl.loop(0, height // 16)
    def _(tile):
        rows = pl.ds(pl.multiple_of(tile * 16, 16), 16)
        out[rows, :] = (
            total[0, SELF, rows, :].astype(jnp.float32)
            + from_z[0, rows, :].astype(jnp.float32)
            + from_z[1, rows, :].astype(jnp.float32)
            + from_z[2, rows, :].astype(jnp.float32)
        )

    sends.finish()


def scatter_grads(grads, small, rows, cols):
    height, width = grads.shape[1] // rows, grads.shape[2]
    if (rows, cols) != (RING_ROWS, RING_COLS):
        flat = grads.reshape(cols * rows * height, width)
        return (
            lax.psum_scatter(flat, ("col", "row"), scatter_dimension=0, tiled=True).astype(
                jnp.float32
            ),
            lax.psum(small, ("row", "col")),
        )
    kind = grads.dtype
    shape = (height, width)
    return pl.pallas_call(
        scatter_kernel,
        out_shape=(
            jax.ShapeDtypeStruct(shape, jnp.float32),
            jax.ShapeDtypeStruct(small.shape, small.dtype),
        ),
        in_specs=[pl.BlockSpec(memory_space=pl.ANY), pl.BlockSpec(memory_space=pltpu.VMEM)],
        out_specs=(
            pl.BlockSpec(memory_space=pltpu.VMEM),
            pl.BlockSpec(memory_space=pltpu.VMEM),
        ),
        scratch_shapes=[
            pltpu.VMEM((cols, 4) + shape, kind),
            pltpu.VMEM((cols, 4) + shape, kind),
            pltpu.VMEM((cols,) + shape, kind),
            pltpu.VMEM((cols,) + shape, kind),
            pltpu.VMEM((cols,) + shape, kind),
            pltpu.VMEM((cols,) + shape, kind),
            pltpu.VMEM((cols - 1,) + shape, kind),
            pltpu.VMEM((5,) + small.shape, small.dtype),
            pltpu.VMEM((5,) + small.shape, small.dtype),
            pltpu.SemaphoreType.DMA((16,)),
            pltpu.SemaphoreType.DMA((SCATTER_COPIES,)),
            pltpu.SemaphoreType.DMA((SCATTER_COPIES,)),
        ],
        compiler_params=pltpu.CompilerParams(
            collective_id=1, has_side_effects=True, vmem_limit_bytes=56 * 2**20
        ),
    )(grads.reshape(cols, rows, height, width), small)


def on_device(
    block_input,
    block_cotangent,
    block_lengths,
    block_offsets,
    norm1_gain,
    norm1_bias,
    norm2_gain,
    norm2_bias,
    qkv_weight,
    qkv_bias,
    dense_weight,
    dense_bias,
    fc_in_weight,
    fc_in_bias,
    fc_out_weight,
    fc_out_bias,
):
    rows = lax.axis_size("row")
    cols = lax.axis_size("col")
    col_index = lax.axis_index("col")
    own_rows = block_input.shape[0]
    width = block_input.shape[1]
    head_dim = width // HEADS
    block_count = block_lengths.shape[0]
    block_rows = own_rows // block_count
    pair_count = block_count // 2
    four_shape = (pair_count, 2 * block_rows, HEADS, head_dim)
    score_scale = head_dim ** (-0.5)
    qkv_cols = qkv_weight.shape[1]
    att_cols = dense_weight.shape[0]
    ff_cols = fc_in_weight.shape[1]
    cuts = (qkv_cols, qkv_cols + att_cols, qkv_cols + att_cols + ff_cols)

    shard = jnp.concatenate([qkv_weight, dense_weight.T, fc_in_weight, fc_out_weight.T], axis=1)
    biases = lax.all_gather(jnp.concatenate([qkv_bias, fc_in_bias]), "col", axis=0, tiled=False)
    qkv_bias_full = biases[:, :qkv_cols].reshape(-1)
    fc_in_bias_full = biases[:, qkv_cols:].reshape(-1)
    gathered = gather_shards(shard, rows, cols)
    qkv_full = gathered[:, :, : cuts[0]]
    dense_full = gathered[:, :, cuts[0] : cuts[1]]
    fc_in_full = gathered[:, :, cuts[1] : cuts[2]]
    fc_out_full = gathered[:, :, cuts[2] :]

    in_block = jnp.arange(block_rows, dtype=jnp.int32)
    positions = (block_offsets[:, None] + in_block[None, :]).reshape(-1)
    valid = (in_block[None, :] < block_lengths[:, None]).reshape(-1)
    cosine, sine_table = rotary_tables(positions, ROT)
    allowed = pair_mask(block_lengths, block_offsets, block_rows)
    standard, inverse = normalize(block_input)
    normed_first = (standard * norm1_gain + norm1_bias).astype(jnp.bfloat16)
    normed_second = (standard * norm2_gain + norm2_bias).astype(jnp.bfloat16)
    grad_out = jnp.where(valid[:, None], block_cotangent, jnp.zeros_like(block_cotangent))

    def widen(left, weight):
        return jnp.einsum("rd,cdw->rcw", left, weight, preferred_element_type=jnp.float32).reshape(
            left.shape[0], -1
        )

    def narrow(left, weight):
        split = left.reshape(left.shape[0], cols, -1)
        return jnp.einsum("rcw,cdw->rd", split, weight, preferred_element_type=jnp.float32)

    def outer(left, right):
        split = right.reshape(right.shape[0], cols, -1)
        return jnp.einsum(
            "rd,rcw->cdw", left, split, preferred_element_type=jnp.float32
        ).astype(jnp.bfloat16)

    mixed = (widen(normed_first, qkv_full) + qkv_bias_full).astype(jnp.bfloat16)
    mixed = mixed.reshape(own_rows, 3, HEADS, head_dim)
    queries = rotate(mixed[:, 0].astype(jnp.float32), cosine, sine_table, ROT).astype(jnp.bfloat16)
    key_rows = rotate(mixed[:, 1].astype(jnp.float32), cosine, sine_table, ROT).astype(jnp.bfloat16)
    queries = queries.reshape(four_shape)
    key_rows = key_rows.reshape(four_shape)
    values = mixed[:, 2].reshape(four_shape)
    scores = masked_scores(queries, key_rows, allowed, score_scale)
    highest = jnp.max(scores, axis=-1, keepdims=True)
    totals = highest + jnp.log(jnp.sum(jnp.exp(scores - highest), axis=-1, keepdims=True))
    probability = jnp.exp(scores - totals)
    weights = probability.astype(jnp.bfloat16)
    attended = jnp.einsum("phij,pjhd->pihd", weights, values, preferred_element_type=jnp.float32)
    attended = attended.astype(jnp.bfloat16).reshape(own_rows, width)
    pre_act = widen(normed_second, fc_in_full) + fc_in_bias_full
    hidden = gelu_exact(pre_act).astype(jnp.bfloat16)
    summed = narrow(attended, dense_full) + narrow(hidden, fc_out_full)
    block_out = block_input.astype(jnp.float32) + dense_bias + fc_out_bias + summed
    grad_pre = (widen(grad_out, fc_out_full) * gelu_slope(pre_act)).astype(jnp.bfloat16)
    grad_att = widen(grad_out, dense_full).astype(jnp.bfloat16).reshape(four_shape)
    grad_probs = jnp.einsum("pihd,pjhd->phij", grad_att, values, preferred_element_type=jnp.float32)
    row_dot = jnp.sum(probability * grad_probs, axis=-1, keepdims=True)
    grad_scores = (probability * (grad_probs - row_dot) * score_scale).astype(jnp.bfloat16)
    grad_query = jnp.einsum(
        "phij,pjhd->pihd", grad_scores, key_rows, preferred_element_type=jnp.float32
    )
    grad_key = jnp.einsum(
        "phij,pihd->pjhd", grad_scores, queries, preferred_element_type=jnp.float32
    )
    grad_values = jnp.einsum(
        "phij,pihd->pjhd", weights, grad_att, preferred_element_type=jnp.float32
    )
    grad_query = unrotate(
        grad_query.reshape(own_rows, HEADS, head_dim), cosine, sine_table, ROT
    ).astype(jnp.bfloat16)
    grad_key = unrotate(
        grad_key.reshape(own_rows, HEADS, head_dim), cosine, sine_table, ROT
    ).astype(jnp.bfloat16)
    grad_values = grad_values.astype(jnp.bfloat16).reshape(own_rows, HEADS, head_dim)
    grad_mixed = jnp.stack([grad_query, grad_key, grad_values], axis=1).reshape(own_rows, 3 * width)
    back_first = narrow(grad_mixed, qkv_full)
    back_second = narrow(grad_pre, fc_in_full)
    input_grad = (
        grad_out.astype(jnp.float32)
        + norm_back(back_first, norm1_gain, standard, inverse)
        + norm_back(back_second, norm2_gain, standard, inverse)
    )
    grads = jnp.concatenate(
        [
            outer(normed_first, grad_mixed),
            outer(grad_out, attended),
            outer(normed_second, grad_pre),
            outer(grad_out, hidden),
        ],
        axis=2,
    )
    small = jnp.concatenate(
        [
            jnp.sum(back_first * standard, axis=0),
            jnp.sum(back_first, axis=0),
            jnp.sum(back_second * standard, axis=0),
            jnp.sum(back_second, axis=0),
            jnp.sum(grad_out, axis=0, dtype=jnp.float32),
            jnp.sum(grad_mixed, axis=0, dtype=jnp.float32),
            jnp.sum(grad_pre, axis=0, dtype=jnp.float32),
        ]
    ).reshape(-1, 128)
    own_grads, small_sum = scatter_grads(grads, small, rows, cols)
    small_sum = small_sum.reshape(-1)
    gain_one, bias_one, gain_two, bias_two, out_bias = (
        small_sum[at * width : (at + 1) * width] for at in range(5)
    )
    qkv_from = 5 * width
    in_from = qkv_from + 3 * width
    qkv_bias_grad = lax.dynamic_slice_in_dim(small_sum, qkv_from + col_index * qkv_cols, qkv_cols, 0)
    fc_in_bias_grad = lax.dynamic_slice_in_dim(small_sum, in_from + col_index * ff_cols, ff_cols, 0)
    return (
        block_out,
        input_grad,
        gain_one,
        bias_one,
        gain_two,
        bias_two,
        own_grads[:, : cuts[0]],
        qkv_bias_grad,
        own_grads[:, cuts[0] : cuts[1]].T,
        out_bias,
        own_grads[:, cuts[1] : cuts[2]],
        fc_in_bias_grad,
        own_grads[:, cuts[2] :].T,
        out_bias,
    )


def solution(mesh):
    return jax.shard_map(
        on_device,
        mesh=mesh,
        in_specs=(
            P(("row", "col"), None),
            P(("row", "col"), None),
            P(("row", "col")),
            P(("row", "col")),
            P(),
            P(),
            P(),
            P(),
            P("row", "col"),
            P("col"),
            P("col", "row"),
            P(),
            P("row", "col"),
            P("col"),
            P("col", "row"),
            P(),
        ),
        out_specs=(
            P(("row", "col"), None),
            P(("row", "col"), None),
            P(),
            P(),
            P(),
            P(),
            P("row", "col"),
            P("col"),
            P("col", "row"),
            P(),
            P("row", "col"),
            P("col"),
            P("col", "row"),
            P(),
        ),
        check_vma=False,
    )
```

```python
import math

import jax
import jax.numpy as jnp
from jax import lax
from jax.experimental import pallas as pl
from jax.experimental.pallas import tpu as pltpu
from jax.sharding import PartitionSpec as P

HEADS = 12
ROT = 16


NORM_EPSILON = 1e-05
HALF_ROOT = math.sqrt(0.5)
DENSITY_SCALE = 1.0 / math.sqrt(2.0 * math.pi)


def normalize(features):
    widened = features.astype(jnp.float32)
    centered = widened - jnp.mean(widened, axis=1, keepdims=True)
    inverse = lax.rsqrt(jnp.mean(centered * centered, axis=1, keepdims=True) + NORM_EPSILON)
    return (centered * inverse, inverse)


def norm_back(grad_normed, gain, standard, inverse):
    grad_unit = grad_normed * gain
    return inverse * (
        grad_unit
        - jnp.mean(grad_unit, axis=1, keepdims=True)
        - standard * jnp.mean(grad_unit * standard, axis=1, keepdims=True)
    )


def gelu_exact(pre_act):
    return 0.5 * pre_act * (1.0 + lax.erf(pre_act * HALF_ROOT))


def gelu_slope(pre_act):
    return (
        0.5 * (1.0 + lax.erf(pre_act * HALF_ROOT))
        + pre_act * jnp.exp(-0.5 * pre_act * pre_act) * DENSITY_SCALE
    )


def rotary_tables(positions, rotated):
    halves = rotated // 2
    frequency = 10000.0 ** (-2.0 * jnp.arange(halves, dtype=jnp.float32) / rotated)
    angles = positions[:, None].astype(jnp.float32) * frequency[None, :]
    angles = jnp.concatenate([angles, angles], axis=1)
    return (jnp.cos(angles)[:, None, :], jnp.sin(angles)[:, None, :])


def rotate(values, cosine, sine_table, rotated):
    halves = rotated // 2
    leading = values[..., :rotated]
    turned = jnp.concatenate([-leading[..., halves:], leading[..., :halves]], axis=-1)
    return jnp.concatenate([leading * cosine + turned * sine_table, values[..., rotated:]], axis=-1)


def unrotate(gradient, cosine, sine_table, rotated):
    halves = rotated // 2
    leading = gradient[..., :rotated]
    scaled = leading * sine_table
    turned = jnp.concatenate([scaled[..., halves:], -scaled[..., :halves]], axis=-1)
    return jnp.concatenate([leading * cosine + turned, gradient[..., rotated:]], axis=-1)


def pair_mask(lengths, offsets, block_rows):
    pair_count = lengths.shape[0] // 2
    local_rows = jnp.arange(2 * block_rows, dtype=jnp.int32)
    block_of = local_rows // block_rows
    in_block = local_rows % block_rows
    pair_lengths = lengths.reshape(pair_count, 2)
    joined = offsets.reshape(pair_count, 2)[:, 1] > 0
    row_limit = jnp.where(block_of[None, :] == 0, pair_lengths[:, 0:1], pair_lengths[:, 1:2])
    live_keys = in_block[None, :] < row_limit
    same_seq = (block_of[:, None] == block_of[None, :])[None, :, :] | joined[:, None, None]
    causal = (local_rows[None, :] <= local_rows[:, None])[None, :, :]
    diagonal = (local_rows[:, None] == local_rows[None, :])[None, :, :]
    return same_seq & causal & (live_keys[:, None, :] | diagonal)


def masked_scores(queries, key_rows, allowed, score_scale):
    scores = (
        jnp.einsum("pihd,pjhd->phij", queries, key_rows, preferred_element_type=jnp.float32)
        * score_scale
    )
    return jnp.where(allowed[:, None, :, :], scores, -jnp.inf)


MESH = pl.DeviceIdType.MESH
RING_ROWS = 8
RING_COLS = 4


def partners():
    row = lax.axis_index("row")
    col = lax.axis_index("col")
    beside = row + 1 - 2 * (row % 2)
    across = row + 2 - 4 * ((row // 2) % 2)
    above = row + 4 - 8 * (row // 4)
    return row, col, beside, across, above


def greet(row, col, beside, across, above):
    barrier = pltpu.get_barrier_semaphore()
    others = [(beside, col), (across, col), (above, col)]
    others += [(row, (col + step) % RING_COLS) for step in range(1, RING_COLS)]
    for other in others:
        pl.semaphore_signal(barrier, inc=1, device_id=other, device_id_type=MESH)
    pl.semaphore_wait(barrier, len(others))


class Sends:
    def __init__(self, send_sems, recv_sems):
        self.send_sems = send_sems
        self.recv_sems = recv_sems
        self.copies = {}

    def start(self, name, source, target, device):
        at = len(self.copies)
        copy = pltpu.make_async_remote_copy(
            src_ref=source,
            dst_ref=target,
            send_sem=self.send_sems.at[at],
            recv_sem=self.recv_sems.at[at],
            device_id=device,
            device_id_type=MESH,
        )
        copy.start()
        self.copies[name] = copy

    def arrived(self, name):
        self.copies[name].wait_recv()

    def finish(self):
        for copy in self.copies.values():
            copy.wait_send()


GATHER_COPIES = 42


def gather_kernel(shard, bias, out, bias_out, own_sem, send_sems, recv_sems):
    row, col, beside, across, above = partners()
    diagonal = across + 4 - 8 * (across // 4)
    half = shard.shape[0] // 2
    low, high = pl.ds(0, half), pl.ds(half, half)
    greet(row, col, beside, across, above)
    sends = Sends(send_sems, recv_sems)
    own = pltpu.make_async_copy(shard, out.at[col, row], own_sem)
    own.start()
    bias_out[col] = bias[...]

    def share(step):
        at = (col - step + RING_COLS) % RING_COLS
        piece = shard if step == 0 else out.at[at, row]
        sends.start(("x", step), piece, out.at[at, row], (across, col))
        sends.start(("y", step), piece, out.at[at, row], (above, col))
        if step == 0:
            for hop in (1, 2, 3):
                there = (col + hop) % RING_COLS
                sends.start(("z", hop), shard, out.at[col, row], (row, there))
                sends.start(("b", hop), bias, bias_out.at[col], (row, there))
        sends.start(("c", step), piece, out.at[at, row], (beside, col))

    def relay(step):
        at = (col - step + RING_COLS) % RING_COLS
        sends.arrived(("x", step))
        sends.start(("dy", step), out.at[at, across, high], out.at[at, across, high], (above, col))
        sends.start(("cx", step), out.at[at, across], out.at[at, across], (beside, col))
        sends.arrived(("y", step))
        sends.start(("dx", step), out.at[at, above, low], out.at[at, above, low], (across, col))
        sends.start(("cy", step), out.at[at, above], out.at[at, above], (beside, col))

    def close(step):
        at = (col - step + RING_COLS) % RING_COLS
        sends.arrived(("dx", step))
        sends.start(("cdx", step), out.at[at, diagonal, low], out.at[at, diagonal, low], (beside, col))
        sends.arrived(("dy", step))
        sends.start(("cdy", step), out.at[at, diagonal, high], out.at[at, diagonal, high], (beside, col))

    share(0)
    sends.arrived(("z", 1))
    share(1)
    relay(0)
    sends.arrived(("z", 2))
    share(2)
    relay(1)
    close(0)
    sends.arrived(("z", 3))
    share(3)
    relay(2)
    close(1)
    relay(3)
    close(2)
    close(3)
    for step in range(RING_COLS):
        for kind in ("c", "cx", "cy", "cdx", "cdy"):
            sends.arrived((kind, step))
    for hop in (1, 2, 3):
        sends.arrived(("b", hop))
    sends.finish()
    own.wait()


def gather_shards(shard, bias, rows, cols):
    if (rows, cols) != (RING_ROWS, RING_COLS):
        return lax.all_gather(shard, ("col", "row"), axis=0, tiled=True).reshape(
            cols, rows * shard.shape[0], shard.shape[1]
        ), lax.all_gather(bias, "col", axis=0, tiled=False)
    gathered, biases = pl.pallas_call(
        gather_kernel,
        out_shape=(
            jax.ShapeDtypeStruct((cols, rows) + shard.shape, shard.dtype),
            jax.ShapeDtypeStruct((cols,) + bias.shape, bias.dtype),
        ),
        in_specs=[pl.BlockSpec(memory_space=pl.ANY), pl.BlockSpec(memory_space=pltpu.VMEM)],
        out_specs=(pl.BlockSpec(memory_space=pl.ANY), pl.BlockSpec(memory_space=pltpu.VMEM)),
        scratch_shapes=[
            pltpu.SemaphoreType.DMA,
            pltpu.SemaphoreType.DMA((GATHER_COPIES,)),
            pltpu.SemaphoreType.DMA((GATHER_COPIES,)),
        ],
        compiler_params=pltpu.CompilerParams(collective_id=0, has_side_effects=True),
    )(shard, bias)
    return gathered.reshape(cols, rows * shard.shape[0], shard.shape[1]), biases


SCATTER_COPIES = 80


def add_rows(target, source, start, count):
    @pl.loop(0, count // 16)
    def _(tile):
        rows = pl.ds(pl.multiple_of(start + tile * 16, 16), 16)
        target[rows, :] = (
            target[rows, :].astype(jnp.float32) + source[rows, :].astype(jnp.float32)
        ).astype(target.dtype)


SELF, ACROSS, ABOVE, DIAGONAL = range(4)


def scatter_kernel(
    grads_att,
    grads_in,
    grads_out,
    small,
    out_att,
    out_in,
    out_out,
    small_out,
    total,
    from_core,
    from_x,
    from_y,
    diag_x,
    diag_y,
    from_z,
    small_in,
    small_sum,
    own_sems,
    send_sems,
    recv_sems,
):
    row, col, beside, across, above = partners()
    diagonal = across + 4 - 8 * (across // 4)
    chips = (row, across, above, diagonal)
    height, part = out_att.shape
    outs = (out_att, out_in, out_out)
    lanes = [pl.ds(at * part, part) for at in range(len(outs))]
    half = height // 2
    low, high = pl.ds(0, half), pl.ds(half, half)
    order = (1, 2, 3, 0)
    places = (DIAGONAL, ACROSS, ABOVE, SELF)
    greet(row, col, beside, across, above)
    sends = Sends(send_sems, recv_sems)
    next_col = col + 1 - 2 * (col % 2)
    far_col = col + 2 - 4 * (col // 2)
    small_targets = ((beside, col), (across, col), (above, col), (row, next_col), (row, far_col))

    def send_small(stage):
        sends.start(("s", stage), small_sum.at[stage], small_in.at[stage], small_targets[stage])

    def fold_small(stage):
        sends.arrived(("s", stage))
        summed = small_sum[stage] + small_in[stage]
        if stage + 1 < len(small_targets):
            small_sum[stage + 1] = summed
            send_small(stage + 1)
        else:
            small_out[...] = summed

    small_sum[0] = small[...]
    loads = {}
    for step in order:
        at = (col + step) % RING_COLS
        for place in places:
            chip = chips[place]
            other = chip + 1 - 2 * (chip % 2)
            columns = pl.ds(pl.multiple_of(at * part, 128), part)
            away = pl.ds(pl.multiple_of(other * height, 16), height)
            kept = pl.ds(pl.multiple_of(chip * height, 16), height)
            for index, grads in enumerate((grads_att, grads_in, grads_out)):
                sends.start(
                    ("c", step, place, index),
                    grads.at[away, columns],
                    from_core.at[step, place, :, lanes[index]],
                    (beside, col),
                )
                load = pltpu.make_async_copy(
                    grads.at[kept, columns],
                    total.at[step, place, :, lanes[index]],
                    own_sems.at[(step * 4 + place) * 3 + index],
                )
                load.start()
                loads[step, place, index] = load
    send_small(0)

    def pair(step):
        for place in places:
            for index in range(len(outs)):
                loads[step, place, index].wait()
                sends.arrived(("c", step, place, index))
            add_rows(total.at[step, place], from_core.at[step, place], 0, height)
            if place == DIAGONAL:
                sends.start(
                    ("dx", step), total.at[step, DIAGONAL, low], diag_x.at[step, low], (across, col)
                )
                sends.start(
                    ("dy", step), total.at[step, DIAGONAL, high], diag_y.at[step, high], (above, col)
                )

    def turn(step):
        sends.arrived(("dx", step))
        add_rows(total.at[step, ABOVE], diag_x.at[step], 0, half)
        sends.start(("y", step), total.at[step, ABOVE], from_y.at[step], (above, col))
        sends.arrived(("dy", step))
        add_rows(total.at[step, ACROSS], diag_y.at[step], half, half)
        sends.start(("x", step), total.at[step, ACROSS], from_x.at[step], (across, col))

    def leave(step):
        sends.arrived(("x", step))
        add_rows(total.at[step, SELF], from_x.at[step], 0, height)
        sends.arrived(("y", step))
        add_rows(total.at[step, SELF], from_y.at[step], 0, height)
        if step > 0:
            there = (col + step) % RING_COLS
            sends.start(("z", step), total.at[step, SELF], from_z.at[step - 1], (row, there))

    for turn_at in range(len(order) + 2):
        if turn_at < len(order):
            pair(order[turn_at])
        if 1 <= turn_at <= len(order):
            turn(order[turn_at - 1])
        if turn_at >= 2:
            leave(order[turn_at - 2])
        if turn_at < len(small_targets):
            fold_small(turn_at)
    for step in (1, 2, 3):
        sends.arrived(("z", step))

    @pl.loop(0, height // 16)
    def _(tile):
        rows = pl.ds(pl.multiple_of(tile * 16, 16), 16)
        for index, out in enumerate(outs):
            out[rows, :] = (
                total[0, SELF, rows, lanes[index]].astype(jnp.float32)
                + from_z[0, rows, lanes[index]].astype(jnp.float32)
                + from_z[1, rows, lanes[index]].astype(jnp.float32)
                + from_z[2, rows, lanes[index]].astype(jnp.float32)
            )

    sends.finish()


def scatter_grads(grads, small, rows, cols):
    height, width = grads[0].shape[0] // rows, grads[0].shape[1] // cols
    if (rows, cols) != (RING_ROWS, RING_COLS):
        own = [
            lax.psum_scatter(
                lax.psum_scatter(
                    grad.reshape(rows * height, cols, width).swapaxes(0, 1),
                    "col",
                    scatter_dimension=0,
                    tiled=False,
                ),
                "row",
                scatter_dimension=0,
                tiled=True,
            ).astype(jnp.float32)
            for grad in grads
        ]
        return (*own, lax.psum(small, ("row", "col")))
    kind = grads[0].dtype
    shape = (height, len(grads) * width)
    return pl.pallas_call(
        scatter_kernel,
        out_shape=(
            *[jax.ShapeDtypeStruct((height, width), jnp.float32)] * len(grads),
            jax.ShapeDtypeStruct(small.shape, small.dtype),
        ),
        in_specs=[pl.BlockSpec(memory_space=pl.ANY)] * len(grads)
        + [pl.BlockSpec(memory_space=pltpu.VMEM)],
        out_specs=(pl.BlockSpec(memory_space=pltpu.VMEM),) * (len(grads) + 1),
        scratch_shapes=[
            pltpu.VMEM((cols, 4) + shape, kind),
            pltpu.VMEM((cols, 4) + shape, kind),
            pltpu.VMEM((cols,) + shape, kind),
            pltpu.VMEM((cols,) + shape, kind),
            pltpu.VMEM((cols,) + shape, kind),
            pltpu.VMEM((cols,) + shape, kind),
            pltpu.VMEM((cols - 1,) + shape, kind),
            pltpu.VMEM((5,) + small.shape, small.dtype),
            pltpu.VMEM((5,) + small.shape, small.dtype),
            pltpu.SemaphoreType.DMA((16 * len(grads),)),
            pltpu.SemaphoreType.DMA((SCATTER_COPIES,)),
            pltpu.SemaphoreType.DMA((SCATTER_COPIES,)),
        ],
        compiler_params=pltpu.CompilerParams(
            collective_id=1, has_side_effects=True, vmem_limit_bytes=56 * 2**20
        ),
    )(*grads, small)


def on_device(
    block_input,
    block_cotangent,
    block_lengths,
    block_offsets,
    norm1_gain,
    norm1_bias,
    norm2_gain,
    norm2_bias,
    qkv_weight,
    qkv_bias,
    dense_weight,
    dense_bias,
    fc_in_weight,
    fc_in_bias,
    fc_out_weight,
    fc_out_bias,
):
    rows = lax.axis_size("row")
    cols = lax.axis_size("col")
    col_index = lax.axis_index("col")
    own_rows = block_input.shape[0]
    width = block_input.shape[1]
    head_dim = width // HEADS
    block_count = block_lengths.shape[0]
    block_rows = own_rows // block_count
    pair_count = block_count // 2
    four_shape = (pair_count, 2 * block_rows, HEADS, head_dim)
    score_scale = head_dim ** (-0.5)
    qkv_cols = qkv_weight.shape[1]
    att_cols = dense_weight.shape[0]
    ff_cols = fc_in_weight.shape[1]
    cuts = (qkv_cols, qkv_cols + att_cols, qkv_cols + att_cols + ff_cols)

    shard = jnp.concatenate([qkv_weight, dense_weight.T, fc_in_weight, fc_out_weight.T], axis=1)
    bias = jnp.concatenate([qkv_bias, fc_in_bias])[None, :]
    gathered, biases = gather_shards(shard, bias, rows, cols)
    qkv_bias_full = biases[:, 0, :qkv_cols].reshape(-1)
    fc_in_bias_full = biases[:, 0, qkv_cols:].reshape(-1)
    qkv_full = gathered[:, :, : cuts[0]]
    dense_full = gathered[:, :, cuts[0] : cuts[1]]
    fc_in_full = gathered[:, :, cuts[1] : cuts[2]]
    fc_out_full = gathered[:, :, cuts[2] :]

    in_block = jnp.arange(block_rows, dtype=jnp.int32)
    positions = (block_offsets[:, None] + in_block[None, :]).reshape(-1)
    valid = (in_block[None, :] < block_lengths[:, None]).reshape(-1)
    cosine, sine_table = rotary_tables(positions, ROT)
    allowed = pair_mask(block_lengths, block_offsets, block_rows)
    standard, inverse = normalize(block_input)
    normed_first = (standard * norm1_gain + norm1_bias).astype(jnp.bfloat16)
    normed_second = (standard * norm2_gain + norm2_bias).astype(jnp.bfloat16)
    grad_out = jnp.where(valid[:, None], block_cotangent, jnp.zeros_like(block_cotangent))

    def widen(left, weight):
        return jnp.einsum("rd,cdw->rcw", left, weight, preferred_element_type=jnp.float32).reshape(
            left.shape[0], -1
        )

    def narrow(left, weight):
        split = left.reshape(left.shape[0], cols, -1)
        return jnp.einsum("rcw,cdw->rd", split, weight, preferred_element_type=jnp.float32)

    def outer(left, right):
        return lax.dot_general(
            left, right, (((0,), (0,)), ((), ())), preferred_element_type=jnp.float32
        ).astype(jnp.bfloat16)

    mixed = (widen(normed_first, qkv_full) + qkv_bias_full).astype(jnp.bfloat16)
    mixed = mixed.reshape(own_rows, 3, HEADS, head_dim)
    queries = rotate(mixed[:, 0].astype(jnp.float32), cosine, sine_table, ROT).astype(jnp.bfloat16)
    key_rows = rotate(mixed[:, 1].astype(jnp.float32), cosine, sine_table, ROT).astype(jnp.bfloat16)
    queries = queries.reshape(four_shape)
    key_rows = key_rows.reshape(four_shape)
    values = mixed[:, 2].reshape(four_shape)
    scores = masked_scores(queries, key_rows, allowed, score_scale)
    highest = jnp.max(scores, axis=-1, keepdims=True)
    totals = highest + jnp.log(jnp.sum(jnp.exp(scores - highest), axis=-1, keepdims=True))
    probability = jnp.exp(scores - totals)
    weights = probability.astype(jnp.bfloat16)
    attended = jnp.einsum("phij,pjhd->pihd", weights, values, preferred_element_type=jnp.float32)
    attended = attended.astype(jnp.bfloat16).reshape(own_rows, width)
    pre_act = widen(normed_second, fc_in_full) + fc_in_bias_full
    hidden = gelu_exact(pre_act).astype(jnp.bfloat16)
    summed = narrow(attended, dense_full) + narrow(hidden, fc_out_full)
    block_out = block_input.astype(jnp.float32) + dense_bias + fc_out_bias + summed
    grad_pre = (widen(grad_out, fc_out_full) * gelu_slope(pre_act)).astype(jnp.bfloat16)
    grad_att = widen(grad_out, dense_full).astype(jnp.bfloat16).reshape(four_shape)
    grad_probs = jnp.einsum("pihd,pjhd->phij", grad_att, values, preferred_element_type=jnp.float32)
    row_dot = jnp.sum(probability * grad_probs, axis=-1, keepdims=True)
    grad_scores = (probability * (grad_probs - row_dot) * score_scale).astype(jnp.bfloat16)
    grad_query = jnp.einsum(
        "phij,pjhd->pihd", grad_scores, key_rows, preferred_element_type=jnp.float32
    )
    grad_key = jnp.einsum(
        "phij,pihd->pjhd", grad_scores, queries, preferred_element_type=jnp.float32
    )
    grad_values = jnp.einsum(
        "phij,pihd->pjhd", weights, grad_att, preferred_element_type=jnp.float32
    )
    grad_query = unrotate(
        grad_query.reshape(own_rows, HEADS, head_dim), cosine, sine_table, ROT
    ).astype(jnp.bfloat16)
    grad_key = unrotate(
        grad_key.reshape(own_rows, HEADS, head_dim), cosine, sine_table, ROT
    ).astype(jnp.bfloat16)
    grad_values = grad_values.astype(jnp.bfloat16).reshape(own_rows, HEADS, head_dim)
    grad_mixed = jnp.stack([grad_query, grad_key, grad_values], axis=1).reshape(own_rows, 3 * width)
    back_first = narrow(grad_mixed, qkv_full)
    back_second = narrow(grad_pre, fc_in_full)
    input_grad = (
        grad_out.astype(jnp.float32)
        + norm_back(back_first, norm1_gain, standard, inverse)
        + norm_back(back_second, norm2_gain, standard, inverse)
    )
    mixed_cols = jnp.pad(
        grad_mixed.reshape(own_rows, cols, qkv_cols), ((0, 0), (0, 0), (0, att_cols))
    ).reshape(own_rows, -1)
    attended_cols = jnp.pad(
        attended.reshape(own_rows, cols, att_cols), ((0, 0), (0, 0), (qkv_cols, 0))
    ).reshape(own_rows, -1)
    grads = (
        outer(
            jnp.concatenate([normed_first, grad_out], axis=0),
            jnp.concatenate([mixed_cols, attended_cols], axis=0),
        ),
        outer(normed_second, grad_pre),
        outer(grad_out, hidden),
    )
    small = jnp.concatenate(
        [
            jnp.sum(back_first * standard, axis=0),
            jnp.sum(back_first, axis=0),
            jnp.sum(back_second * standard, axis=0),
            jnp.sum(back_second, axis=0),
            jnp.sum(grad_out, axis=0, dtype=jnp.float32),
            jnp.sum(grad_mixed, axis=0, dtype=jnp.float32),
            jnp.sum(grad_pre, axis=0, dtype=jnp.float32),
        ]
    ).reshape(-1, 128)
    att_grads, in_grads, out_grads, small_sum = scatter_grads(grads, small, rows, cols)
    small_sum = small_sum.reshape(-1)
    gain_one, bias_one, gain_two, bias_two, out_bias = (
        small_sum[at * width : (at + 1) * width] for at in range(5)
    )
    qkv_from = 5 * width
    in_from = qkv_from + 3 * width
    qkv_bias_grad = lax.dynamic_slice_in_dim(small_sum, qkv_from + col_index * qkv_cols, qkv_cols, 0)
    fc_in_bias_grad = lax.dynamic_slice_in_dim(small_sum, in_from + col_index * ff_cols, ff_cols, 0)
    return (
        block_out,
        input_grad,
        gain_one,
        bias_one,
        gain_two,
        bias_two,
        att_grads[:, :qkv_cols],
        qkv_bias_grad,
        att_grads[:, qkv_cols:].T,
        out_bias,
        in_grads,
        fc_in_bias_grad,
        out_grads.T,
        out_bias,
    )


def solution(mesh):
    return jax.shard_map(
        on_device,
        mesh=mesh,
        in_specs=(
            P(("row", "col"), None),
            P(("row", "col"), None),
            P(("row", "col")),
            P(("row", "col")),
            P(),
            P(),
            P(),
            P(),
            P("row", "col"),
            P("col"),
            P("col", "row"),
            P(),
            P("row", "col"),
            P("col"),
            P("col", "row"),
            P(),
        ),
        out_specs=(
            P(("row", "col"), None),
            P(("row", "col"), None),
            P(),
            P(),
            P(),
            P(),
            P("row", "col"),
            P("col"),
            P("col", "row"),
            P(),
            P("row", "col"),
            P("col"),
            P("col", "row"),
            P(),
        ),
        check_vma=False,
    )
```
